32 devices in a mesh: gz: 8 (over z, x), gy: 2 (over core), gx: 2 (over y).
Axes of the slice: x: 2, y: 2, z: 4, core: 2. Of those that a mesh axis runs over, the one named last changes fastest.
Arguments:
- positions: float32 [2048, 3, 128], P(('gz', 'gy', 'gx')), may hold values from 0 to 4
- velocities: float32 [2048, 3, 128], P(('gz', 'gy', 'gx')), may hold values from -6 to 6
- charges: float32 [2048, 128], P(('gz', 'gy', 'gx')), may hold values from -4 to 4
- atom_types: int32 [2048, 128], P(('gz', 'gy', 'gx')), may hold values from 0 to 15
- type_radius: float32 [16], replicated, may hold values from 0.3 to 1
- tiles: int32 [8192, 2], P(('gz', 'gy', 'gx')), may hold values from 0 to 383
- tile_live: int32 [32], P(('gz', 'gy', 'gx')), may hold values from 32 to 256, as said below
- destinations: int32 [2048, 1], P(('gz', 'gy', 'gx')), may hold values from 0 to 7; in each aligned block of 64 rows (0 to 63, 64 to 127, ...) at most 16 rows name the same one
Outputs:
- forces: float32 [2048, 3, 128], P(('gz', 'gy', 'gx'))
- arrived: float32 [4096, 8, 128], P(('gz', 'gy', 'gx'))
The draws below stay inside these ranges and needn't reach their ends.
Inputs may be any that keep to these rules, and one draw needn't show every extreme that they name: Each device's used tiles are the first tile_live entries of its list; some device uses all 256. `destinations`: among the rows of one device, at most 16 name the same destination; some destination gets exactly 16 from some device.
All inputs are finite; a program needn't handle non-finite values.
Results may differ from the reference program's by a relative error of at most 0.0003.
Values sent between devices are 32-bit elements; how exact they have to be, the bound alone decides.
No kernel may reach another device: no remote copies, remote signals or barrier semaphores. Data moves between devices by JAX's collectives and lax.ppermute only.
A program may use at most 64 MiB of HBM per device.

```python
import math
import jax
import jax.numpy as jnp
import numpy as np
from jax import lax

ATOMS = 128
CL = 64
TILES = 256
NTYPES = 16
STEPS = 2
CAP = 16
NC = 2048
N_GZ = 8
N_GY = 2
N_GX = 2
DEVICES = 32


def draw_tile_live(key, part):
    spread = jax.random.randint(key, (DEVICES,), TILES // 8, TILES + 1)
    busiest = jax.random.randint(jax.random.fold_in(key, 7), (), 0, DEVICES)
    return jnp.where(jnp.arange(DEVICES) == busiest, TILES, spread).astype(jnp.int32)


def place_ends(entries, key, low, top_value):
    spot = [jax.random.randint(jax.random.fold_in(key, axis), (), 0, length) for axis, length in enumerate(entries.shape)]
    widest = entries.shape.index(max(entries.shape))
    next_to = spot[:widest] + [(spot[widest] + 1) % entries.shape[widest]] + spot[widest + 1:]
    return entries.at[tuple(spot)].set(low).at[tuple(next_to)].set(top_value)


def block_scale(key, shape, cuts, low, high):
    def one(dim, shards_of):
        heights = jax.random.uniform(jax.random.fold_in(jax.random.fold_in(key, 6), dim), (shards_of,), jnp.float32, low / len(cuts), high / len(cuts))
        return jnp.repeat(jnp.exp(heights), shape[dim] // shards_of).reshape((-1,) + (1,) * (len(shape) - dim - 1))

    loudness = one(*cuts[0])
    for cut in cuts[1:]:
        loudness = loudness * one(*cut)
    return loudness


def shared_out(own_key, own, number, rows, count, top, limit, slope):
    sequence = jax.random.permutation(own_key, count)
    heavy_load, common = load_shares(count, rows * top, limit, slope, True), load_shares(count, rows * top, limit, slope, False)
    places = jnp.arange(count)

    def named(tallies, offset_by):
        used = int((tallies > 0).sum())
        fixed = max(1, used // 4)
        moved = fixed + (places - fixed + offset_by * (used - fixed)) % max(1, count - fixed)
        return jnp.zeros((count,), jnp.int32).at[sequence[jnp.where(places < fixed, places, moved)]].set(jnp.asarray(tallies, jnp.int32))

    tallies = jnp.where(number % 4 == 0, named(heavy_load, number // 4), named(common, number - number // 4 - 1))
    mixed = jax.random.permutation(jax.random.fold_in(own, 3), count)
    donor, receiver = mixed[0:count // 2 * 2:2], mixed[1:count // 2 * 2:2]
    slack = jnp.minimum(tallies[donor] - 1, limit - tallies[receiver]) // 2
    slack = jnp.where((donor == sequence[0]) | (receiver == sequence[0]) | (tallies[receiver] == 0), 0, jnp.maximum(slack, 0))
    moved = jax.random.randint(jax.random.fold_in(own, 4), (count // 2,), 0, 1 << 20) % (slack + 1)
    tallies = tallies.at[donor].add(-moved).at[receiver].add(moved)
    labels = jnp.searchsorted(jnp.cumsum(tallies), jnp.arange(rows * top), side="right").astype(jnp.int32)
    listing = labels.reshape(top, rows).T
    listing = listing[jax.random.permutation(jax.random.fold_in(own, 1), rows)]
    offset_by = jax.random.randint(jax.random.fold_in(own, 2), (rows, 1), 0, top)
    return jnp.take_along_axis(listing, (jnp.arange(top)[None, :] + offset_by) % top, axis=1)


def load_shares(amount, total, bound, slope, full):
    weights = [(1 << 20) // math.isqrt(standing ** slope) + 1 for standing in range(1, amount + 1)]
    largest = bound if full else min(bound, max(-(-total // amount), total * weights[0] // sum(weights)))
    least = 1 if total - largest >= amount - 1 else 0
    counts, rest = [largest] + [least] * (amount - 1), total - largest - least * (amount - 1)
    while rest > 0:
        free = [i for i in range(1, amount) if counts[i] < largest] or [i for i in range(1, amount) if counts[i] < bound]
        whole, left = sum([weights[i] for i in free]), rest
        for i in free:
            extra = min(bound - counts[i], max(1, left * weights[i] // whole), rest)
            counts[i] = counts[i] + extra
            rest = rest - extra
    return np.array(counts)


def noise(rng, extent, scale, bound, split=(), kind=jnp.bfloat16):
    drawn = scale * jax.random.normal(rng, extent, jnp.float32)
    if split:
        drawn = drawn * block_scale(rng, extent, split, -0.22, 0.18)
    return jnp.clip(drawn, -bound, bound).astype(kind)


def setup_inputs(seed: int = 0) -> dict:
    streams_of = jax.random.split(jax.random.key(seed), 9)
    positions = jnp.clip(4.0 * jax.random.uniform(streams_of[0], (NC, 3, ATOMS), jnp.float32) ** block_scale(streams_of[0], (NC, 3, ATOMS), ((0, 32),), -0.2, 0.2), 0.0, 4.0)
    velocities = noise(streams_of[1], (NC, 3, ATOMS), 1.0, 6.0, ((0, 32),), jnp.float32)
    charges = noise(streams_of[2], (NC, ATOMS), 1.0, 4.0, ((0, 32),), jnp.float32)
    atom_types = place_ends(jax.random.randint(streams_of[3], (NC, ATOMS), 0, NTYPES), jax.random.fold_in(streams_of[3], 1), 0, NTYPES - 1).astype(jnp.int32)
    type_radius = jnp.clip(jnp.exp(jax.random.uniform(streams_of[4], (NTYPES,), jnp.float32, math.log(0.3), math.log(1.0))), 0.3, 1.0)
    tiles = place_ends(jax.random.randint(streams_of[5], (TILES * DEVICES, 2), 0, (N_GY * N_GX + 2) * CL), jax.random.fold_in(streams_of[5], 1), 0, ((N_GY * N_GX + 2) * CL) - 1).astype(jnp.int32)
    tile_live = draw_tile_live(jax.random.fold_in(streams_of[8], 71), 0)
    destinations_keys = jax.random.split(jax.random.fold_in(streams_of[7], 1), NC // CL)
    destinations_turns = jax.random.permutation(jax.random.fold_in(streams_of[7], 3), NC // CL)
    destinations = jax.vmap(lambda own, number: shared_out(jax.random.fold_in(streams_of[7], 2), own, number, CL, N_GZ, 1, CAP, 1))(destinations_keys, destinations_turns).reshape((NC, 1))
    return {"positions": positions, "velocities": velocities, "charges": charges, "atom_types": atom_types, "type_radius": type_radius, "tiles": tiles, "tile_live": tile_live, "destinations": destinations}


coulomb = 0.3
time_step = 0.05
tile_group = 8

def tile_forces(packed, tile_pairs, live_count):
    group_count = tile_pairs.shape[0] // tile_group

    def one_group(group_index, totals):
        first_tile = group_index * tile_group
        chosen = lax.dynamic_slice_in_dim(tile_pairs, first_tile, tile_group, 0)
        left_ids = chosen[:, 0]
        right_ids = chosen[:, 1]
        active = (first_tile + jnp.arange(tile_group, dtype=jnp.int32) < live_count).astype(jnp.float32)
        left_atoms = packed[left_ids]
        right_atoms = packed[right_ids]
        offset = left_atoms[:, 0:3, :, None] - right_atoms[:, 0:3, None, :]
        dist_sq = lax.optimization_barrier(jnp.sum(offset * offset, axis=1))
        soften = left_atoms[:, 4, :, None] + right_atoms[:, 4, None, :]
        denominator = dist_sq + soften * soften
        strength = coulomb * left_atoms[:, 3, :, None] * right_atoms[:, 3, None, :] / (denominator * jnp.sqrt(denominator))
        strength = strength * active[:, None, None]
        pushed = strength[:, None] * offset
        on_left = lax.optimization_barrier(jnp.sum(pushed, axis=3))
        on_right = -lax.optimization_barrier(jnp.sum(pushed, axis=2))
        return totals.at[left_ids].add(on_left).at[right_ids].add(on_right)
    zeros = jnp.zeros((packed.shape[0], 3, packed.shape[2]), jnp.float32)
    return lax.fori_loop(0, group_count, one_group, zeros)

def map_tiles(pieces):
    return tile_forces(pieces[0], pieces[1], pieces[2])

def reference(positions, velocities, charges, atom_types, type_radius, tiles, tile_live, destinations):
    plate_size = N_GY * N_GX
    type_ids = jnp.arange(NTYPES, dtype=jnp.int32)
    atom_radii = lax.optimization_barrier(jnp.sum(jnp.where(atom_types[..., None] == type_ids, type_radius, 0.0), axis=-1))
    tile_pairs = tiles.reshape(DEVICES, TILES, 2)

    def all_forces(places):
        packed = jnp.concatenate([places, charges[:, None], atom_radii[:, None]], axis=1)
        packed = packed.reshape(N_GZ, plate_size, CL, 5, ATOMS)
        plate_rows = jnp.broadcast_to(packed.reshape(N_GZ, 1, plate_size * CL, 5, ATOMS), (N_GZ, plate_size, plate_size * CL, 5, ATOMS))
        lower_block = jnp.roll(packed, 1, axis=0)
        upper_block = jnp.roll(packed, -1, axis=0)
        buffers = jnp.concatenate([plate_rows, lower_block, upper_block], axis=2)
        buffers = buffers.reshape(DEVICES, (plate_size + 2) * CL, 5, ATOMS)
        partial_value = lax.map(map_tiles, (buffers, tile_pairs, tile_live))
        pieces = partial_value.reshape(N_GZ, plate_size, plate_size + 2, CL, 3, ATOMS)
        home_forces = lax.optimization_barrier(jnp.sum(pieces[:, :, :plate_size], axis=1))
        home_forces = home_forces + jnp.roll(pieces[:, :, plate_size], -1, axis=0)
        home_forces = home_forces + jnp.roll(pieces[:, :, plate_size + 1], 1, axis=0)
        return home_forces.reshape(NC, 3, ATOMS)
    places = positions
    moving = velocities
    forces = jnp.zeros_like(positions)
    for step_index in range(STEPS):
        forces = all_forces(places)
        moving = moving + time_step * forces
        places = places + time_step * moving
    carried = jnp.concatenate([places, moving, charges[:, None], atom_radii[:, None]], axis=1)
    carried = carried.reshape(DEVICES, CL, 8, ATOMS)
    target_all = destinations.reshape(DEVICES, CL)
    slot_count = N_GZ * CAP

    def pack_slots(pieces):
        cluster_rows, target_ids = pieces
        onehot = (target_ids[:, None] == jnp.arange(N_GZ, dtype=jnp.int32)[None, :]).astype(jnp.int32)
        rank_before = jnp.cumsum(onehot, axis=0) - onehot
        position = lax.optimization_barrier(jnp.sum(rank_before * onehot, axis=1)) + target_ids * CAP
        select = (position[None, :] == jnp.arange(slot_count, dtype=jnp.int32)[:, None]).astype(jnp.float32)
        return jnp.einsum('sc,cfa->sfa', select, cluster_rows, precision=lax.Precision.HIGHEST)
    sent_slots = lax.map(pack_slots, (carried, target_all))
    sent_slots = sent_slots.reshape(N_GZ, N_GY, N_GX, N_GZ, CAP, 8, ATOMS)
    arrived = jnp.transpose(sent_slots, (3, 1, 2, 0, 4, 5, 6)).reshape(DEVICES * slot_count, 8, ATOMS)
    return (forces, arrived)
```

```python
import functools

import jax
import jax.numpy as jnp
from jax import lax
from jax.experimental import pallas as pl
from jax.experimental.pallas import tpu as pltpu
from jax.sharding import PartitionSpec as P

STEPS = 2

coulomb = 0.3
time_step = 0.05
middle = 2.0
feature_rows = 33
moment_rows = 9
unroll = 16


def shifted(value, axis, steps):
    count = lax.axis_size(axis)
    return lax.ppermute(value, axis, [(i, (i + steps) % count) for i in range(count)])


def rounded(value):
    return value.astype(jnp.bfloat16).astype(jnp.float32)


def tile_kernel(clusters, *refs):
    pairs, live = refs[0:2]
    places = refs[2:8]
    fixed = refs[8:14]
    forces = refs[14:20]
    features, moments, totals, squares, highs, lows, turned_highs, turned_lows = refs[20:28]
    width = features.shape[1]
    ones = jnp.ones((clusters, width), jnp.float32)
    none = jnp.zeros((clusters, width), jnp.float32)
    for piece in range(6):
        first = piece * clusters

        def put(row, value):
            features[pl.ds(first * feature_rows + row, clusters, stride=feature_rows), :] = value

        charge = fixed[piece][3]
        square = none
        for part in range(4):
            value = places[piece][part] - middle if part < 3 else fixed[piece][4]
            square = square + value * value
            high = rounded(value)
            rest = value - high
            mid = rounded(rest)
            low = rounded(rest - mid)
            put(part, high)
            put(4 + part, mid)
            put(8 + part, high)
            put(12 + part, low)
            put(16 + part, high)
            weighed = charge * value if part < 3 else charge
            weighed_high = rounded(weighed)
            base = first * moment_rows + part
            moments[pl.ds(base, clusters, stride=moment_rows), :] = weighed_high
            moments[pl.ds(base + 4, clusters, stride=moment_rows), :] = rounded(weighed - weighed_high)
        high = rounded(square)
        rest = square - high
        mid = rounded(rest)
        for row, value in enumerate((high, mid, rounded(rest - mid), none)):
            put(20 + row, value)
            put(24 + row, ones if row < 3 else none)
            put(28 + row, value)
    totals[...] = jnp.zeros_like(totals)
    squares[...] = jnp.ones_like(squares)
    highs[...] = jnp.zeros_like(highs)
    lows[...] = jnp.zeros_like(lows)
    turned_highs[...] = jnp.zeros_like(highs)
    turned_lows[...] = jnp.zeros_like(lows)
    row = lax.broadcasted_iota(jnp.int32, (24, width), 0) % 4
    scale = jnp.where(row == 3, 2.0, -2.0)
    last = pairs.shape[0] // 2 - 1

    def ends(t):
        t = jnp.clip(t, 0, last)
        return pairs[2 * t], pairs[2 * t + 1]

    def features_of(t):
        left, right = ends(t)
        left_base = left * feature_rows
        right_base = right * feature_rows
        pair_a = features[pl.ds(left_base, 8), :]
        streamed = jnp.concatenate([pair_a, pair_a, features[pl.ds(left_base + 8, 8), :]], axis=0) * scale
        streamed = jnp.concatenate([streamed, features[pl.ds(left_base + 20, 8), :]], axis=0)
        kept = jnp.concatenate(
            [
                features[pl.ds(right_base, 8), :],
                features[pl.ds(right_base + 4, 8), :],
                features[pl.ds(right_base + 12, 8), :],
                features[pl.ds(right_base + 24, 8), :],
            ],
            axis=0,
        )
        return streamed.astype(jnp.bfloat16), kept.astype(jnp.bfloat16)

    def prepared(t):
        streamed, kept = zip(features_of(t), features_of(t + 1))
        apart = jnp.zeros_like(kept[0])
        kept = jnp.concatenate(
            [jnp.concatenate([kept[0], apart], axis=1), jnp.concatenate([apart, kept[1]], axis=1)], axis=0
        )
        return jnp.concatenate(streamed, axis=0).T, kept

    def distances(streamed, kept, slot):
        square = lax.dot_general(
            streamed,
            kept,
            (((1,), (0,)), ((), ())),
            preferred_element_type=jnp.float32,
        )
        squares[slot] = square[:, :width]
        squares[slot + 1] = square[:, width:]

    def strengths(slot):
        inverse = lax.rsqrt(squares[slot])
        strength = inverse * inverse * inverse
        high = strength.astype(jnp.bfloat16)
        low = (strength - high.astype(jnp.float32)).astype(jnp.bfloat16)
        highs[slot] = high
        lows[slot] = low
        turned_highs[slot] = high.T
        turned_lows[slot] = low.T

    def pushes(t, slot):
        left, right = ends(t)
        left_at = left * moment_rows
        right_at = right * moment_rows
        weight = jnp.where((t >= 0) & (t < live[0]), 1.0, 0.0)
        both = jnp.concatenate([moments[pl.ds(left_at, 8), :], moments[pl.ds(right_at, 8), :]], axis=0)
        both = (both * weight).astype(jnp.bfloat16)
        turned = jnp.concatenate([turned_highs[slot], turned_lows[slot]], axis=1)
        straight = jnp.concatenate([highs[slot], lows[slot]], axis=1)
        on_left = jnp.dot(both, turned, preferred_element_type=jnp.float32)
        on_right = jnp.dot(both, straight, preferred_element_type=jnp.float32)
        on_left = on_left[8:]
        on_right = on_right[:8]
        return left_at, right_at, on_left[:, :width] + on_left[:, width:], on_right[:, :width] + on_right[:, width:]

    def group(g, carry):
        first = g * unroll
        ready = [prepared(first + u) for u in range(0, unroll, 2)]
        pushed = [pushes(first + u - 2 * unroll, u) for u in range(unroll)]
        for u in range(unroll):
            strengths(u)
        for u in range(0, unroll, 2):
            distances(*ready[u // 2], u)
        for left_at, right_at, on_left, on_right in pushed:
            totals[pl.ds(left_at, 8), :] += on_left
            totals[pl.ds(right_at, 8), :] += on_right
        return carry

    lax.fori_loop(0, (live[0] + unroll - 1) // unroll + 2, group, 0)
    for piece in range(6):
        first = piece * clusters * moment_rows

        def total(row):
            return (
                totals[pl.ds(first + row, clusters, stride=moment_rows), :]
                + totals[pl.ds(first + row + 4, clusters, stride=moment_rows), :]
            )

        charge = coulomb * fixed[piece][3]
        summed = total(3)
        for part in range(3):
            forces[piece][part] = charge * ((places[piece][part] - middle) * summed - total(part))


def tile_forces(pairs, live, places, fixed):
    _, clusters, width = places[0].shape
    smem = pl.BlockSpec(memory_space=pltpu.SMEM)
    vmem = pl.BlockSpec(memory_space=pltpu.VMEM)
    return pl.pallas_call(
        functools.partial(tile_kernel, clusters),
        out_shape=[jax.ShapeDtypeStruct((3, clusters, width), jnp.float32)] * 6,
        in_specs=[smem, smem] + [vmem] * 12,
        out_specs=[vmem] * 6,
        scratch_shapes=[
            pltpu.VMEM((6 * clusters * feature_rows, width), jnp.float32),
            pltpu.VMEM((6 * clusters * moment_rows, width), jnp.float32),
            pltpu.VMEM((6 * clusters * moment_rows, width), jnp.float32),
            pltpu.VMEM((unroll, width, width), jnp.float32),
            pltpu.VMEM((unroll, width, width), jnp.bfloat16),
            pltpu.VMEM((unroll, width, width), jnp.bfloat16),
            pltpu.VMEM((unroll, width, width), jnp.bfloat16),
            pltpu.VMEM((unroll, width, width), jnp.bfloat16),
        ],
        compiler_params=pltpu.CompilerParams(vmem_limit_bytes=40 << 20),
        name="tile_forces",
    )(pairs, live, *places, *fixed)


def imported(value):
    over_x = shifted(value, "gx", 1)
    return [
        value,
        over_x,
        shifted(value, "gy", 1),
        shifted(over_x, "gy", 1),
        shifted(value, "gz", 1),
        shifted(value, "gz", -1),
    ]


def returned(partial):
    below = shifted(partial[4], "gz", -1)
    above = shifted(partial[5], "gz", 1)
    direct = shifted(partial[2], "gy", 1)
    beyond = shifted(partial[3], "gy", 1)
    across = shifted(partial[1] + beyond, "gx", 1)
    return partial[0] + direct + across + below + above


def local(positions, velocities, charges, atom_types, type_radius, tiles, tile_live, destinations):
    clusters = positions.shape[0]
    width = positions.shape[2]
    type_ids = jnp.arange(type_radius.shape[0], dtype=jnp.int32)
    atom_radii = jnp.sum(jnp.where(atom_types[..., None] == type_ids, type_radius, 0.0), axis=-1)
    mine = lax.axis_index("gy") * lax.axis_size("gx") + lax.axis_index("gx")
    block = tiles // clusters
    block = jnp.where(block < 4, block ^ mine, block)
    pairs = (block * clusters + tiles % clusters).reshape(-1)
    places = jnp.transpose(positions, (1, 0, 2))
    moving = jnp.transpose(velocities, (1, 0, 2))
    home = jnp.concatenate([places, charges[None], atom_radii[None]], axis=0)
    fixed = imported(home)
    current = fixed
    for step_index in range(STEPS):
        if step_index:
            current = imported(places)
        forces = returned(tile_forces(pairs, tile_live, current, fixed))
        moving = moving + time_step * forces
        places = places + time_step * moving
    carried = jnp.concatenate([places, moving, charges[None], atom_radii[None]], axis=0)
    groups = lax.axis_size("gz")
    capacity = max(2, 2 * clusters // groups)
    slot_count = groups * capacity
    target_ids = destinations[:, 0]
    onehot = (target_ids[:, None] == jnp.arange(groups, dtype=jnp.int32)[None, :]).astype(jnp.int32)
    rank_before = jnp.cumsum(onehot, axis=0) - onehot
    position = jnp.sum(rank_before * onehot, axis=1) + target_ids * capacity
    select = (position[None, :] == jnp.arange(slot_count, dtype=jnp.int32)[:, None]).astype(jnp.float32)
    sent_slots = jnp.einsum("sc,fca->sfa", select, carried, precision=lax.Precision.HIGHEST)
    received = lax.all_to_all(
        sent_slots.reshape(groups, capacity, 8, width), "gz", split_axis=0, concat_axis=0, tiled=True
    )
    return (jnp.transpose(forces, (1, 0, 2)), received.reshape(slot_count, 8, width))


def solution(mesh):
    whole = ("gz", "gy", "gx")
    placed = (
        P(whole, None, None),
        P(whole, None, None),
        P(whole, None),
        P(whole, None),
        P(),
        P(whole, None),
        P(whole),
        P(whole, None),
    )
    return jax.shard_map(
        local,
        mesh=mesh,
        in_specs=placed,
        out_specs=(P(whole, None, None), P(whole, None, None)),
        check_vma=False,
    )
```

```python
import functools

import jax
import jax.numpy as jnp
from jax import lax
from jax.experimental import pallas as pl
from jax.experimental.pallas import tpu as pltpu
from jax.sharding import PartitionSpec as P


STEPS = 2

coulomb = 0.3
time_step = 0.05
middle = 2.0
feature_rows = 33
moment_rows = 9
half = 16
pair_bits = 9
pair_base = 1 << pair_bits


def shifted(value, axis, steps):
    count = lax.axis_size(axis)
    return lax.ppermute(value, axis, [(i, (i + steps) % count) for i in range(count)])


def rounded(value):
    return value.astype(jnp.bfloat16).astype(jnp.float32)


def tile_kernel(clusters, tiles, *refs):
    pairs = refs[0]
    places = refs[1:7]
    fixed = refs[7:13]
    forces = refs[13:19]
    features, moments, totals = refs[19:22]
    even, odd = refs[22:27], refs[27:32]
    live = pairs[tiles]
    width = features.shape[1]
    ones = jnp.ones((clusters, width), jnp.float32)
    none = jnp.zeros((clusters, width), jnp.float32)
    for piece in range(6):
        first = piece * clusters

        def put(row, value):
            features[pl.ds(first * feature_rows + row, clusters, stride=feature_rows), :] = value

        charge = fixed[piece][3 * clusters : 4 * clusters, :]
        square = none
        for part in range(4):
            value = places[piece][part * clusters : (part + 1) * clusters, :] - middle if part < 3 else fixed[piece][4 * clusters : 5 * clusters, :]
            square = square + value * value
            high = rounded(value)
            rest = value - high
            mid = rounded(rest)
            low = rounded(rest - mid)
            put(part, high)
            put(4 + part, mid)
            put(8 + part, high)
            put(12 + part, low)
            put(16 + part, high)
            weighed = charge * value if part < 3 else charge
            weighed_high = rounded(weighed)
            base = first * moment_rows + part
            moments[pl.ds(base, clusters, stride=moment_rows), :] = weighed_high
            moments[pl.ds(base + 4, clusters, stride=moment_rows), :] = rounded(weighed - weighed_high)
        high = rounded(square)
        rest = square - high
        mid = rounded(rest)
        for row, value in enumerate((high, mid, rounded(rest - mid), none)):
            put(20 + row, value)
            put(24 + row, ones if row < 3 else none)
            put(28 + row, value)
    totals[...] = jnp.zeros_like(totals)
    row = lax.broadcasted_iota(jnp.int32, (24, width), 0) % 4
    scale = jnp.where(row == 3, 2.0, -2.0)

    def ends(t):
        pair = pairs[jnp.minimum(t, tiles - 1)]
        return pair >> pair_bits, pair & (pair_base - 1)

    def features_of(t):
        left, right = ends(t)
        left_base = left * feature_rows
        right_base = right * feature_rows
        pair_a = features[pl.ds(left_base, 8), :]
        streamed = jnp.concatenate([pair_a, pair_a, features[pl.ds(left_base + 8, 8), :]], axis=0) * scale
        streamed = jnp.concatenate([streamed, features[pl.ds(left_base + 20, 8), :]], axis=0)
        kept = jnp.concatenate(
            [
                features[pl.ds(right_base, 8), :],
                features[pl.ds(right_base + 4, 8), :],
                features[pl.ds(right_base + 12, 8), :],
                features[pl.ds(right_base + 24, 8), :],
            ],
            axis=0,
        )
        return streamed.astype(jnp.bfloat16), kept.astype(jnp.bfloat16)

    def prepared(t):
        streamed, kept = zip(features_of(t), features_of(t + 1))
        apart = jnp.zeros_like(kept[0])
        kept = jnp.concatenate(
            [jnp.concatenate([kept[0], apart], axis=1), jnp.concatenate([apart, kept[1]], axis=1)], axis=0
        )
        return jnp.concatenate(streamed, axis=0).T, kept

    def distances(streamed, kept, squares, slot):
        square = lax.dot_general(
            streamed,
            kept,
            (((1,), (0,)), ((), ())),
            preferred_element_type=jnp.float32,
        )
        squares[slot] = square[:, :width]
        squares[slot + 1] = square[:, width:]

    def strengths(squares, kept, slot):
        inverse = lax.rsqrt(squares[slot])
        strength = inverse * inverse * inverse
        high = strength.astype(jnp.bfloat16)
        low = (strength - high.astype(jnp.float32)).astype(jnp.bfloat16)
        for ref, value in zip(kept, (high, low, high.T, low.T)):
            ref[slot] = value

    def pushes(t, kept, slot):
        left, right = ends(t)
        left_at = left * moment_rows
        right_at = right * moment_rows
        active = t < live
        both = jnp.concatenate([moments[pl.ds(left_at, 8), :], moments[pl.ds(right_at, 8), :]], axis=0)
        both = both.astype(jnp.bfloat16)
        high, low, turned_high, turned_low = [ref[slot] for ref in kept]
        turned = jnp.concatenate([turned_high, turned_low], axis=1)
        straight = jnp.concatenate([high, low], axis=1)
        on_left = jnp.dot(both, turned, preferred_element_type=jnp.float32)[8:]
        on_right = jnp.dot(both, straight, preferred_element_type=jnp.float32)[:8]
        on_left = jnp.where(active, on_left[:, :width] + on_left[:, width:], 0.0)
        on_right = jnp.where(active, on_right[:, :width] + on_right[:, width:], 0.0)
        return left_at, right_at, on_left, on_right

    def phase(number, now, other, filling=0):
        first = number * half
        ready = [prepared(first + u) for u in range(0, half, 2)]
        pushed = [] if filling else [pushes(first + u - 2 * half, now[1:], u) for u in range(half)]
        if filling != 2:
            for u in range(half):
                strengths(other[0], other[1:], u)
        for u in range(0, half, 2):
            distances(*ready[u // 2], now[0], u)
        for left_at, right_at, on_left, on_right in pushed:
            totals[pl.ds(left_at, 8), :] += on_left
            totals[pl.ds(right_at, 8), :] += on_right

    def group(g, carry):
        phase(2 * g, even, odd)
        phase(2 * g + 1, odd, even)
        return carry

    phase(0, even, odd, filling=2)
    phase(1, odd, even, filling=1)
    lax.fori_loop(1, 1 + (live + 2 * half - 1) // (2 * half), group, 0)
    for piece in range(6):
        first = piece * clusters * moment_rows

        def total(row):
            return (
                totals[pl.ds(first + row, clusters, stride=moment_rows), :]
                + totals[pl.ds(first + row + 4, clusters, stride=moment_rows), :]
            )

        charge = coulomb * fixed[piece][3 * clusters : 4 * clusters, :]
        summed = total(3)
        for part in range(3):
            forces[piece][part * clusters : (part + 1) * clusters, :] = charge * ((places[piece][part * clusters : (part + 1) * clusters, :] - middle) * summed - total(part))


def tile_forces(pairs, tiles, clusters, places, fixed):
    width = places[0].shape[1]
    smem = pl.BlockSpec(memory_space=pltpu.SMEM)
    vmem = pl.BlockSpec(memory_space=pltpu.VMEM)
    stage = [pltpu.VMEM((half, width, width), jnp.float32)] + [pltpu.VMEM((half, width, width), jnp.bfloat16)] * 4
    return pl.pallas_call(
        functools.partial(tile_kernel, clusters, tiles),
        out_shape=[jax.ShapeDtypeStruct((3 * clusters, width), jnp.float32)] * 6,
        in_specs=[smem] + [vmem] * 12,
        out_specs=[vmem] * 6,
        scratch_shapes=[
            pltpu.VMEM((6 * clusters * feature_rows, width), jnp.float32),
            pltpu.VMEM((6 * clusters * moment_rows, width), jnp.float32),
            pltpu.VMEM((6 * clusters * moment_rows, width), jnp.float32),
        ]
        + stage * 2,
        compiler_params=pltpu.CompilerParams(vmem_limit_bytes=28 << 20),
        cost_estimate=pl.CostEstimate(flops=1 << 33, bytes_accessed=1 << 22, transcendentals=1 << 22),
        name="tile_forces",
    )(pairs, *places, *fixed)


def home_kernel(clusters, lists, places, charges, types, radii, tiles, live, home):
    width = charges.shape[1]
    home[0 : 3 * clusters, :] = places[...]
    home[3 * clusters : 4 * clusters, :] = charges[...]
    radius = jnp.zeros(types.shape, jnp.float32)
    for kind in range(radii.shape[0]):
        radius = jnp.where(types[...] == kind, radii[kind], radius)
    home[4 * clusters : 5 * clusters, :] = radius
    first = 5 * clusters
    for side in range(2):
        for row in range(lists):
            part = tiles[side : side + 1, row * width : (row + 1) * width]
            home[pl.ds(first + side * lists + row, 1), :] = part.astype(jnp.float32)
    rest = home.shape[0] - first - 2 * lists
    home[pl.ds(first + 2 * lists, rest), :] = jnp.full((rest, width), live[0]).astype(jnp.float32)


def home_array(places, charges, types, radii, tiles, live):
    clusters, width = charges.shape
    lists = tiles.shape[1] // width
    extra = -(-(2 * lists + 1) // 8) * 8
    smem = pl.BlockSpec(memory_space=pltpu.SMEM)
    vmem = pl.BlockSpec(memory_space=pltpu.VMEM)
    return pl.pallas_call(
        functools.partial(home_kernel, clusters, lists),
        out_shape=jax.ShapeDtypeStruct((5 * clusters + extra, width), jnp.float32),
        in_specs=[vmem, vmem, vmem, smem, vmem, smem],
        out_specs=vmem,
        name="home_array",
    )(places, charges, types, radii, tiles, live)


def plan_kernel(clusters, lists, mine, *refs):
    pieces, plan = refs[:4], refs[4]
    width = plan.shape[1]
    tiles = lists * width
    first = 5 * clusters
    me = mine[0]
    lane = lax.broadcasted_iota(jnp.int32, (lists, width), 1)
    place = (lax.broadcasted_iota(jnp.int32, (lists, width), 0) * width + lane).astype(jnp.float32)
    source = lax.broadcasted_iota(jnp.int32, (width, width), 0)
    target = lax.broadcasted_iota(jnp.int32, (width, width), 1)
    before = jnp.where(source < target, 1.0, 0.0).astype(jnp.bfloat16)

    def ranked(mask):
        inside = jnp.dot(mask.astype(jnp.bfloat16), before, preferred_element_type=jnp.float32)
        counts = [jnp.sum(mask[row : row + 1]) for row in range(lists)]
        return inside, counts

    sides, shared, towers = [], [], []
    for piece in pieces:
        left = piece[pl.ds(first, lists), :]
        right = piece[pl.ds(first + lists, lists), :]
        used = place < piece[pl.ds(first + 2 * lists, 1), :]
        plate = jnp.maximum(left, right) < 4 * clusters
        sides.append((left, right))
        shared.append(jnp.where(used & plate, 1.0, 0.0))
        towers.append(jnp.where(used & ~plate, 1.0, 0.0))
    ranks = [ranked(mask) for mask in shared]
    plates = [sum(counts) for _, counts in ranks]
    tower_counts = [jnp.sum(mask) for mask in towers]
    total = sum(plates)

    def filled(level):
        return sum([jnp.maximum(level - count, 0.0) for count in tower_counts])

    level = jnp.float32(0.0)
    step = 1
    while step < 2 * tiles:
        step *= 2
    while step >= 1:
        level = jnp.where(filled(level + step) < total, level + step, level)
        step //= 2
    shares = [jnp.maximum(level + 1.0 - count, 0.0) for count in tower_counts]

    def ahead(values, index):
        here = me ^ index
        return sum([jnp.where((me ^ other) < here, value, 0.0) for other, value in enumerate(values)])

    begin = jnp.minimum(ahead(shares, 0), total)
    end = jnp.minimum(ahead(shares, 0) + shares[0], total)
    taken = end - begin
    slot_index = lax.broadcasted_iota(jnp.int32, (tiles, width), 0).astype(jnp.float32)
    row_index = lax.broadcasted_iota(jnp.int32, (8, width), 0)
    chosen = jnp.zeros((8, tiles), jnp.float32)
    own_inside, own_counts = ranked(towers[0])
    for index in range(4):
        inside, counts = ranks[index]
        base = ahead(plates, index)
        own_base = taken
        for row in range(lists):
            slot = inside[row : row + 1] + (base - begin)
            mine_now = (shared[index][row : row + 1] > 0.5) & (slot > -0.5) & (slot < taken - 0.5)
            slot = jnp.where(mine_now, slot, -1.0)
            base = base + counts[row]
            if index == 0:
                slot = jnp.where(towers[0][row : row + 1] > 0.5, own_inside[row : row + 1] + own_base, slot)
                own_base = own_base + own_counts[row]
            values = jnp.zeros((8, width), jnp.float32)
            for side in range(2):
                rows = sides[index][side][row : row + 1]
                block = jnp.floor((rows + 0.5) * (1.0 / clusters))
                within = rows - block * clusters
                whole = block.astype(jnp.int32)
                moved = jnp.where(whole < 4, whole ^ me, whole).astype(jnp.float32)
                values = jnp.where(row_index == 2 * side, moved, values)
                values = jnp.where(row_index == 2 * side + 1, within, values)
            hits = jnp.where(slot_index == slot, 1.0, 0.0).astype(jnp.bfloat16)
            chosen += lax.dot_general(
                values.astype(jnp.bfloat16), hits, (((1,), (1,)), ((), ())), preferred_element_type=jnp.float32
            )
    whole_row = lax.broadcasted_iota(jnp.int32, (8, tiles), 0)
    scales = (float(clusters * pair_base), float(pair_base), float(clusters), 1.0)
    scale = jnp.zeros((8, tiles), jnp.float32)
    for row, value in enumerate(scales):
        scale = jnp.where(whole_row == row, value, scale)
    packed = jnp.sum(chosen * scale, axis=0, keepdims=True).astype(jnp.int32)
    count = (taken + tower_counts[0]).astype(jnp.int32)
    for row in range(lists):
        plan[row : row + 1, :] = packed[:, row * width : (row + 1) * width]
    plan[pl.ds(lists, plan.shape[0] - lists), :] = jnp.full((plan.shape[0] - lists, width), count)


def planned(mine, clusters, tiles, pieces):
    width = pieces[0].shape[1]
    lists = tiles // width
    smem = pl.BlockSpec(memory_space=pltpu.SMEM)
    vmem = pl.BlockSpec(memory_space=pltpu.VMEM)
    plan = pl.pallas_call(
        functools.partial(plan_kernel, clusters, lists),
        out_shape=jax.ShapeDtypeStruct((-(-(lists + 1) // 8) * 8, width), jnp.int32),
        in_specs=[smem] + [vmem] * 4,
        out_specs=vmem,
        compiler_params=pltpu.CompilerParams(vmem_limit_bytes=8 << 20),
        name="plan",
    )(mine.reshape(1), *pieces)
    return plan.reshape(-1)


def imported(value):
    below = shifted(value, "gz", 1)
    above = shifted(value, "gz", -1)
    over_x = shifted(value, "gx", 1)
    over_y = shifted(value, "gy", 1)
    beyond = shifted(over_x, "gy", 1)
    return [value, over_x, over_y, beyond, below, above]


def returned(partial):
    below = shifted(partial[4], "gz", -1)
    above = shifted(partial[5], "gz", 1)
    direct = shifted(partial[2], "gy", 1)
    beyond = shifted(partial[3], "gy", 1)
    across = shifted(partial[1] + beyond, "gx", 1)
    return partial[0] + direct + across + below + above


def local(positions, velocities, charges, atom_types, type_radius, tiles, tile_live, destinations):
    clusters = positions.shape[0]
    width = positions.shape[2]
    mine = lax.axis_index("gy") * lax.axis_size("gx") + lax.axis_index("gx")
    tile_count = tiles.shape[0]
    places = jnp.transpose(positions, (1, 0, 2)).reshape(3 * clusters, width)
    moving = jnp.transpose(velocities, (1, 0, 2)).reshape(3 * clusters, width)
    home = home_array(places, charges, atom_types, type_radius, jnp.transpose(tiles), tile_live)
    steady = home[3 * clusters : 5 * clusters]
    groups = lax.axis_size("gz")
    capacity = max(2, 2 * clusters // groups)
    slot_count = groups * capacity
    target_ids = destinations[:, 0]
    onehot = (target_ids[:, None] == jnp.arange(groups, dtype=jnp.int32)[None, :]).astype(jnp.int32)
    rank_before = jnp.cumsum(onehot, axis=0) - onehot
    position = jnp.sum(rank_before * onehot, axis=1) + target_ids * capacity
    select = (position[None, :] == jnp.arange(slot_count, dtype=jnp.int32)[:, None]).astype(jnp.float32)

    def migrated(channels):
        count = channels.shape[0] // clusters
        channels = channels.reshape(count, clusters, width)
        slots = jnp.einsum("sc,fca->fsa", select, channels, precision=lax.Precision.HIGHEST)
        slots = jnp.transpose(slots.reshape(count, groups, capacity, width), (1, 0, 2, 3))
        received = lax.all_to_all(slots, "gz", split_axis=0, concat_axis=0, tiled=True)
        return jnp.transpose(received, (1, 0, 2, 3)).reshape(count, slot_count, width)

    fixed = imported(home)
    pairs = planned(mine, clusters, tile_count, fixed[:4])
    current = fixed
    for step_index in range(STEPS):
        if step_index:
            current = imported(places)
            sent = migrated(jnp.concatenate([places, moving, steady], axis=0))
        forces = returned(tile_forces(pairs, tile_count, clusters, current, fixed))
        if not step_index:
            moving = moving + time_step * forces
            places = places + time_step * moving
    pushed = migrated(forces)
    moved = sent[3:6] + time_step * pushed
    placed = sent[0:3] + time_step * moved
    arrived = jnp.concatenate([placed, moved, sent[6:]], axis=0)
    return (jnp.transpose(forces.reshape(3, clusters, width), (1, 0, 2)), jnp.transpose(arrived, (1, 0, 2)))


def solution(mesh):
    whole = ("gz", "gy", "gx")
    placed = (
        P(whole, None, None),
        P(whole, None, None),
        P(whole, None),
        P(whole, None),
        P(),
        P(whole, None),
        P(whole),
        P(whole, None),
    )
    return jax.shard_map(
        local,
        mesh=mesh,
        in_specs=placed,
        out_specs=(P(whole, None, None), P(whole, None, None)),
        check_vma=False,
    )
```

```python
import functools

import jax
import jax.numpy as jnp
from jax import lax
from jax.experimental import pallas as pl
from jax.experimental.pallas import tpu as pltpu
from jax.sharding import PartitionSpec as P


STEPS = 2

coulomb = 0.3
time_step = 0.05
middle = 2.0
least_square = 0.3599
feature_rows = 33
moment_rows = 9
half = 16
pair_bits = 9
pair_base = 1 << pair_bits


def shifted(value, axis, steps):
    count = lax.axis_size(axis)
    return lax.ppermute(value, axis, [(i, (i + steps) % count) for i in range(count)])


def rounded(value):
    return value.astype(jnp.bfloat16).astype(jnp.float32)


def tile_kernel(clusters, tiles, *refs):
    pairs = refs[0]
    places = refs[1:7]
    fixed = refs[7:13]
    forces = refs[13:19]
    features, moments, totals = refs[19:22]
    even, odd = refs[22:27], refs[27:32]
    live = pairs[tiles]
    width = features.shape[1]
    ones = jnp.ones((clusters, width), jnp.float32)
    none = jnp.zeros((clusters, width), jnp.float32)
    for piece in range(6):
        first = piece * clusters

        def put(row, value):
            features[pl.ds(first * feature_rows + row, clusters, stride=feature_rows), :] = value

        charge = fixed[piece][3 * clusters : 4 * clusters, :]
        square = none
        for part in range(4):
            value = places[piece][part * clusters : (part + 1) * clusters, :] - middle if part < 3 else fixed[piece][4 * clusters : 5 * clusters, :]
            square = square + value * value
            high = rounded(value)
            rest = value - high
            mid = rounded(rest)
            low = rounded(rest - mid)
            put(part, high)
            put(4 + part, mid)
            put(8 + part, high)
            put(12 + part, low)
            put(16 + part, high)
            weighed = charge * value if part < 3 else charge
            weighed_high = rounded(weighed)
            base = first * moment_rows + part
            moments[pl.ds(base, clusters, stride=moment_rows), :] = weighed_high
            moments[pl.ds(base + 4, clusters, stride=moment_rows), :] = rounded(weighed - weighed_high)
        high = rounded(square)
        rest = square - high
        mid = rounded(rest)
        for row, value in enumerate((high, mid, rounded(rest - mid), none)):
            put(20 + row, value)
            put(24 + row, ones if row < 3 else none)
            put(28 + row, value)
    totals[...] = jnp.zeros_like(totals)
    row = lax.broadcasted_iota(jnp.int32, (24, width), 0) % 4
    scale = jnp.where(row == 3, 2.0, -2.0)

    def ends(t):
        pair = pairs[jnp.minimum(t, tiles - 1)]
        return pair >> pair_bits, pair & (pair_base - 1)

    def features_of(t):
        left, right = ends(t)
        left_base = left * feature_rows
        right_base = right * feature_rows
        pair_a = features[pl.ds(left_base, 8), :]
        streamed = jnp.concatenate([pair_a, pair_a, features[pl.ds(left_base + 8, 8), :]], axis=0) * scale
        streamed = jnp.concatenate([streamed, features[pl.ds(left_base + 20, 8), :]], axis=0)
        kept = jnp.concatenate(
            [
                features[pl.ds(right_base, 8), :],
                features[pl.ds(right_base + 4, 8), :],
                features[pl.ds(right_base + 12, 8), :],
                features[pl.ds(right_base + 24, 8), :],
            ],
            axis=0,
        )
        return streamed.astype(jnp.bfloat16), kept.astype(jnp.bfloat16)

    def prepared(t):
        streamed, kept = zip(features_of(t), features_of(t + 1))
        apart = jnp.zeros_like(kept[0])
        kept = jnp.concatenate(
            [jnp.concatenate([kept[0], apart], axis=1), jnp.concatenate([apart, kept[1]], axis=1)], axis=0
        )
        return jnp.concatenate(streamed, axis=0).T, kept

    def distances(streamed, kept, squares, slot):
        square = lax.dot_general(
            streamed,
            kept,
            (((1,), (0,)), ((), ())),
            preferred_element_type=jnp.float32,
        )
        squares[slot] = square[:, :width]
        squares[slot + 1] = square[:, width:]

    def strengths(squares, kept, slot):
        inverse = lax.rsqrt(jnp.maximum(squares[slot], least_square))
        strength = inverse * inverse * inverse
        high = strength.astype(jnp.bfloat16)
        low = (strength - high.astype(jnp.float32)).astype(jnp.bfloat16)
        for ref, value in zip(kept, (high, low, high.T, low.T)):
            ref[slot] = value

    def pushes(t, kept, slot):
        left, right = ends(t)
        left_at = left * moment_rows
        right_at = right * moment_rows
        active = t < live
        both = jnp.concatenate([moments[pl.ds(left_at, 8), :], moments[pl.ds(right_at, 8), :]], axis=0)
        both = both.astype(jnp.bfloat16)
        high, low, turned_high, turned_low = [ref[slot] for ref in kept]
        turned = jnp.concatenate([turned_high, turned_low], axis=1)
        straight = jnp.concatenate([high, low], axis=1)
        on_left = jnp.dot(both, turned, preferred_element_type=jnp.float32)[8:]
        on_right = jnp.dot(both, straight, preferred_element_type=jnp.float32)[:8]
        on_left = jnp.where(active, on_left[:, :width] + on_left[:, width:], 0.0)
        on_right = jnp.where(active, on_right[:, :width] + on_right[:, width:], 0.0)
        return left_at, right_at, on_left, on_right

    def phase(number, now, other, filling=0):
        first = number * half
        ready = [prepared(first + u) for u in range(0, half, 2)]
        pushed = [] if filling else [pushes(first + u - 2 * half, now[1:], u) for u in range(half)]
        if filling != 2:
            for u in range(half):
                strengths(other[0], other[1:], u)
        for u in range(0, half, 2):
            distances(*ready[u // 2], now[0], u)
        for left_at, right_at, on_left, on_right in pushed:
            totals[pl.ds(left_at, 8), :] += on_left
            totals[pl.ds(right_at, 8), :] += on_right

    def group(g, carry):
        phase(2 * g, even, odd)
        phase(2 * g + 1, odd, even)
        return carry

    phase(0, even, odd, filling=2)
    phase(1, odd, even, filling=1)
    lax.fori_loop(1, 1 + (live + 2 * half - 1) // (2 * half), group, 0)
    for piece in range(6):
        first = piece * clusters * moment_rows

        def total(row):
            return (
                totals[pl.ds(first + row, clusters, stride=moment_rows), :]
                + totals[pl.ds(first + row + 4, clusters, stride=moment_rows), :]
            )

        charge = coulomb * fixed[piece][3 * clusters : 4 * clusters, :]
        summed = total(3)
        for part in range(3):
            forces[piece][part * clusters : (part + 1) * clusters, :] = charge * ((places[piece][part * clusters : (part + 1) * clusters, :] - middle) * summed - total(part))


def tile_forces(pairs, tiles, clusters, places, fixed):
    width = places[0].shape[1]
    smem = pl.BlockSpec(memory_space=pltpu.SMEM)
    vmem = pl.BlockSpec(memory_space=pltpu.VMEM)
    stage = [pltpu.VMEM((half, width, width), jnp.float32)] + [pltpu.VMEM((half, width, width), jnp.bfloat16)] * 4
    return pl.pallas_call(
        functools.partial(tile_kernel, clusters, tiles),
        out_shape=[jax.ShapeDtypeStruct((3 * clusters, width), jnp.float32)] * 6,
        in_specs=[smem] + [vmem] * 12,
        out_specs=[vmem] * 6,
        scratch_shapes=[
            pltpu.VMEM((6 * clusters * feature_rows, width), jnp.float32),
            pltpu.VMEM((6 * clusters * moment_rows, width), jnp.float32),
            pltpu.VMEM((6 * clusters * moment_rows, width), jnp.float32),
        ]
        + stage * 2,
        compiler_params=pltpu.CompilerParams(vmem_limit_bytes=28 << 20),
        cost_estimate=pl.CostEstimate(flops=1 << 33, bytes_accessed=1 << 22, transcendentals=1 << 22),
        name="tile_forces",
    )(pairs, *places, *fixed)


def home_kernel(clusters, lists, places, charges, types, radii, tiles, live, home):
    width = charges.shape[1]
    home[0 : 3 * clusters, :] = places[...]
    home[3 * clusters : 4 * clusters, :] = charges[...]
    radius = jnp.zeros(types.shape, jnp.float32)
    for kind in range(radii.shape[0]):
        radius = jnp.where(types[...] == kind, radii[kind], radius)
    home[4 * clusters : 5 * clusters, :] = radius
    first = 5 * clusters
    for side in range(2):
        for row in range(lists):
            part = tiles[side : side + 1, row * width : (row + 1) * width]
            home[pl.ds(first + side * lists + row, 1), :] = part.astype(jnp.float32)
    rest = home.shape[0] - first - 2 * lists
    home[pl.ds(first + 2 * lists, rest), :] = jnp.full((rest, width), live[0]).astype(jnp.float32)


def home_array(places, charges, types, radii, tiles, live):
    clusters, width = charges.shape
    lists = tiles.shape[1] // width
    extra = -(-(2 * lists + 1) // 8) * 8
    smem = pl.BlockSpec(memory_space=pltpu.SMEM)
    vmem = pl.BlockSpec(memory_space=pltpu.VMEM)
    return pl.pallas_call(
        functools.partial(home_kernel, clusters, lists),
        out_shape=jax.ShapeDtypeStruct((5 * clusters + extra, width), jnp.float32),
        in_specs=[vmem, vmem, vmem, smem, vmem, smem],
        out_specs=vmem,
        name="home_array",
    )(places, charges, types, radii, tiles, live)


def plan_kernel(clusters, lists, mine, *refs):
    pieces, plan = refs[:4], refs[4]
    width = plan.shape[1]
    tiles = lists * width
    first = 5 * clusters
    me, flip = mine[0], mine[1]
    lane = lax.broadcasted_iota(jnp.int32, (lists, width), 1)
    place = (lax.broadcasted_iota(jnp.int32, (lists, width), 0) * width + lane).astype(jnp.float32)
    source = lax.broadcasted_iota(jnp.int32, (width, width), 0)
    target = lax.broadcasted_iota(jnp.int32, (width, width), 1)
    before = jnp.where(source < target, 1.0, 0.0).astype(jnp.bfloat16)

    def ranked(mask):
        inside = jnp.dot(mask.astype(jnp.bfloat16), before, preferred_element_type=jnp.float32)
        counts = [jnp.sum(mask[row : row + 1]) for row in range(lists)]
        return inside, counts

    sides, shared, towers = [], [], []
    for piece in pieces:
        left = piece[pl.ds(first, lists), :]
        right = piece[pl.ds(first + lists, lists), :]
        used = place < piece[pl.ds(first + 2 * lists, 1), :]
        plate = jnp.maximum(left, right) < 4 * clusters
        sides.append((left, right))
        shared.append(jnp.where(used & plate, 1.0, 0.0))
        towers.append(jnp.where(used & ~plate, 1.0, 0.0))
    ranks = [ranked(mask) for mask in shared]
    plates = [sum(counts) for _, counts in ranks]
    tower_counts = [jnp.sum(mask) for mask in towers]
    total = sum(plates)

    def filled(level):
        return sum([jnp.maximum(level - count, 0.0) for count in tower_counts])

    level = jnp.float32(0.0)
    step = 1
    while step < 2 * tiles:
        step *= 2
    while step >= 1:
        level = jnp.where(filled(level + step) < total, level + step, level)
        step //= 2
    shares = [jnp.maximum(level + 1.0 - count, 0.0) for count in tower_counts]

    def ahead(values, index):
        here = me ^ index
        return sum([jnp.where((me ^ other) < here, value, 0.0) for other, value in enumerate(values)])

    begin = jnp.minimum(ahead(shares, 0), total)
    end = jnp.minimum(ahead(shares, 0) + shares[0], total)
    taken = end - begin
    slot_index = lax.broadcasted_iota(jnp.int32, (tiles, width), 0).astype(jnp.float32)
    row_index = lax.broadcasted_iota(jnp.int32, (8, width), 0)
    chosen = jnp.zeros((8, tiles), jnp.float32)
    own_inside, own_counts = ranked(towers[0])
    for index in range(4):
        inside, counts = ranks[index]
        base = ahead(plates, index)
        own_base = taken
        for row in range(lists):
            slot = inside[row : row + 1] + (base - begin)
            mine_now = (shared[index][row : row + 1] > 0.5) & (slot > -0.5) & (slot < taken - 0.5)
            slot = jnp.where(mine_now, slot, -1.0)
            base = base + counts[row]
            if index == 0:
                slot = jnp.where(towers[0][row : row + 1] > 0.5, own_inside[row : row + 1] + own_base, slot)
                own_base = own_base + own_counts[row]
            values = jnp.zeros((8, width), jnp.float32)
            for side in range(2):
                rows = sides[index][side][row : row + 1]
                block = jnp.floor((rows + 0.5) * (1.0 / clusters))
                within = rows - block * clusters
                whole = block.astype(jnp.int32)
                moved = jnp.where(whole < 4, whole ^ me, whole ^ flip).astype(jnp.float32)
                values = jnp.where(row_index == 2 * side, moved, values)
                values = jnp.where(row_index == 2 * side + 1, within, values)
            hits = jnp.where(slot_index == slot, 1.0, 0.0).astype(jnp.bfloat16)
            chosen += lax.dot_general(
                values.astype(jnp.bfloat16), hits, (((1,), (1,)), ((), ())), preferred_element_type=jnp.float32
            )
    whole_row = lax.broadcasted_iota(jnp.int32, (8, tiles), 0)
    scales = (float(clusters * pair_base), float(pair_base), float(clusters), 1.0)
    scale = jnp.zeros((8, tiles), jnp.float32)
    for row, value in enumerate(scales):
        scale = jnp.where(whole_row == row, value, scale)
    packed = jnp.sum(chosen * scale, axis=0, keepdims=True).astype(jnp.int32)
    count = (taken + tower_counts[0]).astype(jnp.int32)
    for row in range(lists):
        plan[row : row + 1, :] = packed[:, row * width : (row + 1) * width]
    plan[pl.ds(lists, plan.shape[0] - lists), :] = jnp.full((plan.shape[0] - lists, width), count)


def planned(mine, clusters, tiles, pieces):
    width = pieces[0].shape[1]
    lists = tiles // width
    smem = pl.BlockSpec(memory_space=pltpu.SMEM)
    vmem = pl.BlockSpec(memory_space=pltpu.VMEM)
    plan = pl.pallas_call(
        functools.partial(plan_kernel, clusters, lists),
        out_shape=jax.ShapeDtypeStruct((-(-(lists + 1) // 8) * 8, width), jnp.int32),
        in_specs=[smem] + [vmem] * 4,
        out_specs=vmem,
        compiler_params=pltpu.CompilerParams(vmem_limit_bytes=8 << 20),
        name="plan",
    )(mine, *pieces)
    return plan.reshape(-1)


def paired(value, first):
    count = lax.axis_size("gz")
    pairs = []
    for low in range(first, count, 2):
        pairs += [(low, (low + 1) % count), ((low + 1) % count, low)]
    return lax.ppermute(value, "gz", pairs)


def imported(value):
    below = paired(value, 0)
    above = paired(value, 1)
    over_x = shifted(value, "gx", 1)
    over_y = shifted(value, "gy", 1)
    beyond = shifted(over_x, "gy", 1)
    return [value, over_x, over_y, beyond, below, above]


def returned(partial):
    below = paired(partial[4], 0)
    above = paired(partial[5], 1)
    direct = shifted(partial[2], "gy", 1)
    beyond = shifted(partial[3], "gy", 1)
    across = shifted(partial[1] + beyond, "gx", 1)
    return partial[0] + direct + across + below + above


def local(positions, velocities, charges, atom_types, type_radius, tiles, tile_live, destinations):
    clusters = positions.shape[0]
    width = positions.shape[2]
    plate_place = lax.axis_index("gy") * lax.axis_size("gx") + lax.axis_index("gx")
    mine = jnp.stack([plate_place, 1 - lax.axis_index("gz") % 2])
    tile_count = tiles.shape[0]
    places = jnp.transpose(positions, (1, 0, 2)).reshape(3 * clusters, width)
    moving = jnp.transpose(velocities, (1, 0, 2)).reshape(3 * clusters, width)
    home = home_array(places, charges, atom_types, type_radius, jnp.transpose(tiles), tile_live)
    steady = home[3 * clusters : 5 * clusters]
    groups = lax.axis_size("gz")
    capacity = max(2, 2 * clusters // groups)
    slot_count = groups * capacity
    target_ids = destinations[:, 0]
    onehot = (target_ids[:, None] == jnp.arange(groups, dtype=jnp.int32)[None, :]).astype(jnp.int32)
    rank_before = jnp.cumsum(onehot, axis=0) - onehot
    position = jnp.sum(rank_before * onehot, axis=1) + target_ids * capacity
    select = (position[None, :] == jnp.arange(slot_count, dtype=jnp.int32)[:, None]).astype(jnp.float32)

    def migrated(channels):
        count = channels.shape[0] // clusters
        channels = channels.reshape(count, clusters, width)
        slots = jnp.einsum("sc,fca->fsa", select, channels, precision=lax.Precision.HIGHEST)
        slots = jnp.transpose(slots.reshape(count, groups, capacity, width), (1, 0, 2, 3))
        received = lax.all_to_all(slots, "gz", split_axis=0, concat_axis=0, tiled=True)
        return jnp.transpose(received, (1, 0, 2, 3)).reshape(count, slot_count, width)

    fixed = imported(home)
    pairs = planned(mine, clusters, tile_count, fixed[:4])
    current = fixed
    for step_index in range(STEPS):
        if step_index:
            current = imported(places)
            sent = migrated(jnp.concatenate([places, moving, steady], axis=0))
        forces = returned(tile_forces(pairs, tile_count, clusters, current, fixed))
        if not step_index:
            moving = moving + time_step * forces
            places = places + time_step * moving
    pushed = migrated(forces)
    moved = sent[3:6] + time_step * pushed
    placed = sent[0:3] + time_step * moved
    arrived = jnp.concatenate([placed, moved, sent[6:]], axis=0)
    return (jnp.transpose(forces.reshape(3, clusters, width), (1, 0, 2)), jnp.transpose(arrived, (1, 0, 2)))


def solution(mesh):
    whole = ("gz", "gy", "gx")
    placed = (
        P(whole, None, None),
        P(whole, None, None),
        P(whole, None),
        P(whole, None),
        P(),
        P(whole, None),
        P(whole),
        P(whole, None),
    )
    return jax.shard_map(
        local,
        mesh=mesh,
        in_specs=placed,
        out_specs=(P(whole, None, None), P(whole, None, None)),
        check_vma=False,
    )
```

```python
import functools

import jax
import jax.numpy as jnp
from jax import lax
from jax.experimental import pallas as pl
from jax.experimental.pallas import tpu as pltpu
from jax.sharding import PartitionSpec as P


STEPS = 2

coulomb = 0.3
time_step = 0.05
middle = 2.0
least_square = 0.3599
feature_rows = 33
moment_rows = 9
half = 16
pair_bits = 9
pair_base = 1 << pair_bits


def shifted(value, axis, steps):
    count = lax.axis_size(axis)
    return lax.ppermute(value, axis, [(i, (i + steps) % count) for i in range(count)])


def rounded(value):
    return value.astype(jnp.bfloat16).astype(jnp.float32)


def tile_kernel(clusters, tiles, *refs):
    pairs = refs[0]
    places = refs[1:7]
    fixed = refs[7:13]
    forces = refs[13:19]
    features, moments, totals = refs[19:22]
    even, odd = refs[22:27], refs[27:32]
    live = pairs[tiles]
    width = features.shape[1]
    ones = jnp.ones((clusters, width), jnp.float32)
    none = jnp.zeros((clusters, width), jnp.float32)
    for piece in range(6):
        first = piece * clusters

        def put(row, value):
            features[pl.ds(first * feature_rows + row, clusters, stride=feature_rows), :] = value

        charge = fixed[piece][3 * clusters : 4 * clusters, :]
        square = none
        for part in range(4):
            value = places[piece][part * clusters : (part + 1) * clusters, :] - middle if part < 3 else fixed[piece][4 * clusters : 5 * clusters, :]
            square = square + value * value
            high = rounded(value)
            rest = value - high
            mid = rounded(rest)
            low = rounded(rest - mid)
            put(part, high)
            put(4 + part, mid)
            put(8 + part, high)
            put(12 + part, low)
            put(16 + part, high)
            weighed = charge * value if part < 3 else charge
            weighed_high = rounded(weighed)
            base = first * moment_rows + part
            moments[pl.ds(base, clusters, stride=moment_rows), :] = weighed_high
            moments[pl.ds(base + 4, clusters, stride=moment_rows), :] = rounded(weighed - weighed_high)
        high = rounded(square)
        rest = square - high
        mid = rounded(rest)
        for row, value in enumerate((high, mid, rounded(rest - mid), none)):
            put(20 + row, value)
            put(24 + row, ones if row < 3 else none)
            put(28 + row, value)
    totals[...] = jnp.zeros_like(totals)
    row = lax.broadcasted_iota(jnp.int32, (24, width), 0) % 4
    scale = jnp.where(row == 3, 2.0, -2.0)

    def ends(t):
        pair = pairs[jnp.minimum(t, tiles - 1)]
        return pair >> pair_bits, pair & (pair_base - 1)

    def features_of(t):
        left, right = ends(t)
        left_base = left * feature_rows
        right_base = right * feature_rows
        pair_a = features[pl.ds(left_base, 8), :]
        streamed = jnp.concatenate([pair_a, pair_a, features[pl.ds(left_base + 8, 8), :]], axis=0) * scale
        streamed = jnp.concatenate([streamed, features[pl.ds(left_base + 20, 8), :]], axis=0)
        kept = jnp.concatenate(
            [
                features[pl.ds(right_base, 8), :],
                features[pl.ds(right_base + 4, 8), :],
                features[pl.ds(right_base + 12, 8), :],
                features[pl.ds(right_base + 24, 8), :],
            ],
            axis=0,
        )
        return streamed.astype(jnp.bfloat16), kept.astype(jnp.bfloat16)

    def prepared(t):
        streamed, kept = zip(features_of(t), features_of(t + 1))
        apart = jnp.zeros_like(kept[0])
        kept = jnp.concatenate(
            [jnp.concatenate([kept[0], apart], axis=1), jnp.concatenate([apart, kept[1]], axis=1)], axis=0
        )
        return jnp.concatenate(streamed, axis=0).T, kept

    def distances(streamed, kept, squares, slot):
        square = lax.dot_general(
            streamed,
            kept,
            (((1,), (0,)), ((), ())),
            preferred_element_type=jnp.float32,
        )
        squares[slot] = square[:, :width]
        squares[slot + 1] = square[:, width:]

    def strengths(squares, kept, slot):
        inverse = lax.rsqrt(jnp.maximum(squares[slot], least_square))
        strength = inverse * inverse * inverse
        high = strength.astype(jnp.bfloat16)
        low = (strength - high.astype(jnp.float32)).astype(jnp.bfloat16)
        for ref, value in zip(kept, (high, low, high.T, low.T)):
            ref[slot] = value

    def pushes(t, kept, slot):
        left, right = ends(t)
        left_at = left * moment_rows
        right_at = right * moment_rows
        active = t < live
        both = jnp.concatenate([moments[pl.ds(left_at, 8), :], moments[pl.ds(right_at, 8), :]], axis=0)
        both = both.astype(jnp.bfloat16)
        high, low, turned_high, turned_low = [ref[slot] for ref in kept]
        turned = jnp.concatenate([turned_high, turned_low], axis=1)
        straight = jnp.concatenate([high, low], axis=1)
        on_left = jnp.dot(both, turned, preferred_element_type=jnp.float32)[8:]
        on_right = jnp.dot(both, straight, preferred_element_type=jnp.float32)[:8]
        on_left = jnp.where(active, on_left[:, :width] + on_left[:, width:], 0.0)
        on_right = jnp.where(active, on_right[:, :width] + on_right[:, width:], 0.0)
        return left_at, right_at, on_left, on_right

    def phase(number, now, other, filling=0):
        first = number * half
        ready = [prepared(first + u) for u in range(0, half, 2)]
        pushed = [] if filling else [pushes(first + u - 2 * half, now[1:], u) for u in range(half)]
        if filling != 2:
            for u in range(half):
                strengths(other[0], other[1:], u)
        for u in range(0, half, 2):
            distances(*ready[u // 2], now[0], u)
        for left_at, right_at, on_left, on_right in pushed:
            totals[pl.ds(left_at, 8), :] += on_left
            totals[pl.ds(right_at, 8), :] += on_right

    def group(g, carry):
        phase(2 * g, even, odd)
        phase(2 * g + 1, odd, even)
        return carry

    phase(0, even, odd, filling=2)
    phase(1, odd, even, filling=1)
    groups = (live + half - 1) // half
    lax.fori_loop(1, 1 + groups // 2, group, 0)

    @pl.when(groups % 2 == 1)
    def _():
        final = [pushes((groups - 1) * half + u, even[1:], u) for u in range(half)]
        for left_at, right_at, on_left, on_right in final:
            totals[pl.ds(left_at, 8), :] += on_left
            totals[pl.ds(right_at, 8), :] += on_right

    for piece in range(6):
        first = piece * clusters * moment_rows

        def total(row):
            return (
                totals[pl.ds(first + row, clusters, stride=moment_rows), :]
                + totals[pl.ds(first + row + 4, clusters, stride=moment_rows), :]
            )

        charge = coulomb * fixed[piece][3 * clusters : 4 * clusters, :]
        summed = total(3)
        for part in range(3):
            forces[piece][part * clusters : (part + 1) * clusters, :] = charge * ((places[piece][part * clusters : (part + 1) * clusters, :] - middle) * summed - total(part))


def tile_forces(pairs, tiles, clusters, places, fixed):
    width = places[0].shape[1]
    smem = pl.BlockSpec(memory_space=pltpu.SMEM)
    vmem = pl.BlockSpec(memory_space=pltpu.VMEM)
    stage = [pltpu.VMEM((half, width, width), jnp.float32)] + [pltpu.VMEM((half, width, width), jnp.bfloat16)] * 4
    return pl.pallas_call(
        functools.partial(tile_kernel, clusters, tiles),
        out_shape=[jax.ShapeDtypeStruct((3 * clusters, width), jnp.float32)] * 6,
        in_specs=[smem] + [vmem] * 12,
        out_specs=[vmem] * 6,
        scratch_shapes=[
            pltpu.VMEM((6 * clusters * feature_rows, width), jnp.float32),
            pltpu.VMEM((6 * clusters * moment_rows, width), jnp.float32),
            pltpu.VMEM((6 * clusters * moment_rows, width), jnp.float32),
        ]
        + stage * 2,
        compiler_params=pltpu.CompilerParams(vmem_limit_bytes=28 << 20),
        cost_estimate=pl.CostEstimate(flops=1 << 33, bytes_accessed=1 << 22, transcendentals=1 << 22),
        name="tile_forces",
    )(pairs, *places, *fixed)


def home_kernel(clusters, lists, places, charges, types, radii, tiles, live, home):
    width = charges.shape[1]
    home[0 : 3 * clusters, :] = places[...]
    home[3 * clusters : 4 * clusters, :] = charges[...]
    radius = jnp.zeros(types.shape, jnp.float32)
    for kind in range(radii.shape[0]):
        radius = jnp.where(types[...] == kind, radii[kind], radius)
    home[4 * clusters : 5 * clusters, :] = radius
    first = 5 * clusters
    for side in range(2):
        for row in range(lists):
            part = tiles[side : side + 1, row * width : (row + 1) * width]
            home[pl.ds(first + side * lists + row, 1), :] = part.astype(jnp.float32)
    rest = home.shape[0] - first - 2 * lists
    home[pl.ds(first + 2 * lists, rest), :] = jnp.full((rest, width), live[0]).astype(jnp.float32)


def home_array(places, charges, types, radii, tiles, live):
    clusters, width = charges.shape
    lists = tiles.shape[1] // width
    extra = -(-(2 * lists + 1) // 8) * 8
    smem = pl.BlockSpec(memory_space=pltpu.SMEM)
    vmem = pl.BlockSpec(memory_space=pltpu.VMEM)
    return pl.pallas_call(
        functools.partial(home_kernel, clusters, lists),
        out_shape=jax.ShapeDtypeStruct((5 * clusters + extra, width), jnp.float32),
        in_specs=[vmem, vmem, vmem, smem, vmem, smem],
        out_specs=vmem,
        name="home_array",
    )(places, charges, types, radii, tiles, live)


def plan_kernel(clusters, lists, mine, *refs):
    pieces, plan = refs[:4], refs[4]
    width = plan.shape[1]
    tiles = lists * width
    first = 5 * clusters
    me, flip = mine[0], mine[1]
    lane = lax.broadcasted_iota(jnp.int32, (lists, width), 1)
    place = (lax.broadcasted_iota(jnp.int32, (lists, width), 0) * width + lane).astype(jnp.float32)
    source = lax.broadcasted_iota(jnp.int32, (width, width), 0)
    target = lax.broadcasted_iota(jnp.int32, (width, width), 1)
    before = jnp.where(source < target, 1.0, 0.0).astype(jnp.bfloat16)

    def ranked(mask):
        inside = jnp.dot(mask.astype(jnp.bfloat16), before, preferred_element_type=jnp.float32)
        counts = [jnp.sum(mask[row : row + 1]) for row in range(lists)]
        return inside, counts

    sides, shared, towers = [], [], []
    for piece in pieces:
        left = piece[pl.ds(first, lists), :]
        right = piece[pl.ds(first + lists, lists), :]
        used = place < piece[pl.ds(first + 2 * lists, 1), :]
        plate = jnp.maximum(left, right) < 4 * clusters
        sides.append((left, right))
        shared.append(jnp.where(used & plate, 1.0, 0.0))
        towers.append(jnp.where(used & ~plate, 1.0, 0.0))
    ranks = [ranked(mask) for mask in shared]
    plates = [sum(counts) for _, counts in ranks]
    tower_counts = [jnp.sum(mask) for mask in towers]
    total = sum(plates)

    def filled(level):
        return sum([jnp.maximum(level - count, 0.0) for count in tower_counts])

    level = jnp.float32(0.0)
    step = 1
    while step < 2 * tiles:
        step *= 2
    while step >= 1:
        level = jnp.where(filled(level + step) < total, level + step, level)
        step //= 2
    shares = [jnp.maximum(level + 1.0 - count, 0.0) for count in tower_counts]

    def ahead(values, index):
        here = me ^ index
        return sum([jnp.where((me ^ other) < here, value, 0.0) for other, value in enumerate(values)])

    begin = jnp.minimum(ahead(shares, 0), total)
    end = jnp.minimum(ahead(shares, 0) + shares[0], total)
    taken = end - begin
    slot_index = lax.broadcasted_iota(jnp.int32, (tiles, width), 0).astype(jnp.float32)
    row_index = lax.broadcasted_iota(jnp.int32, (8, width), 0)
    chosen = jnp.zeros((8, tiles), jnp.float32)
    own_inside, own_counts = ranked(towers[0])
    for index in range(4):
        inside, counts = ranks[index]
        base = ahead(plates, index)
        own_base = taken
        for row in range(lists):
            slot = inside[row : row + 1] + (base - begin)
            mine_now = (shared[index][row : row + 1] > 0.5) & (slot > -0.5) & (slot < taken - 0.5)
            slot = jnp.where(mine_now, slot, -1.0)
            base = base + counts[row]
            if index == 0:
                slot = jnp.where(towers[0][row : row + 1] > 0.5, own_inside[row : row + 1] + own_base, slot)
                own_base = own_base + own_counts[row]
            values = jnp.zeros((8, width), jnp.float32)
            for side in range(2):
                rows = sides[index][side][row : row + 1]
                block = jnp.floor((rows + 0.5) * (1.0 / clusters))
                within = rows - block * clusters
                whole = block.astype(jnp.int32)
                moved = jnp.where(whole < 4, whole ^ me, whole ^ flip).astype(jnp.float32)
                values = jnp.where(row_index == 2 * side, moved, values)
                values = jnp.where(row_index == 2 * side + 1, within, values)
            hits = jnp.where(slot_index == slot, 1.0, 0.0).astype(jnp.bfloat16)
            chosen += lax.dot_general(
                values.astype(jnp.bfloat16), hits, (((1,), (1,)), ((), ())), preferred_element_type=jnp.float32
            )
    whole_row = lax.broadcasted_iota(jnp.int32, (8, tiles), 0)
    scales = (float(clusters * pair_base), float(pair_base), float(clusters), 1.0)
    scale = jnp.zeros((8, tiles), jnp.float32)
    for row, value in enumerate(scales):
        scale = jnp.where(whole_row == row, value, scale)
    packed = jnp.sum(chosen * scale, axis=0, keepdims=True).astype(jnp.int32)
    count = (taken + tower_counts[0]).astype(jnp.int32)
    for row in range(lists):
        plan[row : row + 1, :] = packed[:, row * width : (row + 1) * width]
    plan[pl.ds(lists, plan.shape[0] - lists), :] = jnp.full((plan.shape[0] - lists, width), count)


def planned(mine, clusters, tiles, pieces):
    width = pieces[0].shape[1]
    lists = tiles // width
    smem = pl.BlockSpec(memory_space=pltpu.SMEM)
    vmem = pl.BlockSpec(memory_space=pltpu.VMEM)
    plan = pl.pallas_call(
        functools.partial(plan_kernel, clusters, lists),
        out_shape=jax.ShapeDtypeStruct((-(-(lists + 1) // 8) * 8, width), jnp.int32),
        in_specs=[smem] + [vmem] * 4,
        out_specs=vmem,
        compiler_params=pltpu.CompilerParams(vmem_limit_bytes=8 << 20),
        name="plan",
    )(mine, *pieces)
    return plan.reshape(-1)


def paired(value, first):
    count = lax.axis_size("gz")
    pairs = []
    for low in range(first, count, 2):
        pairs += [(low, (low + 1) % count), ((low + 1) % count, low)]
    return lax.ppermute(value, "gz", pairs)


def imported(value):
    below = paired(value, 0)
    above = paired(value, 1)
    over_x = shifted(value, "gx", 1)
    over_y = shifted(value, "gy", 1)
    beyond = shifted(over_x, "gy", 1)
    return [value, over_x, over_y, beyond, below, above]


def returned(partial):
    below = paired(partial[4], 0)
    above = paired(partial[5], 1)
    direct = shifted(partial[2], "gy", 1)
    beyond = shifted(partial[3], "gy", 1)
    across = shifted(partial[1] + beyond, "gx", 1)
    return partial[0] + direct + across + below + above


def local(positions, velocities, charges, atom_types, type_radius, tiles, tile_live, destinations):
    clusters = positions.shape[0]
    width = positions.shape[2]
    plate_place = lax.axis_index("gy") * lax.axis_size("gx") + lax.axis_index("gx")
    mine = jnp.stack([plate_place, 1 - lax.axis_index("gz") % 2])
    tile_count = tiles.shape[0]
    places = jnp.transpose(positions, (1, 0, 2)).reshape(3 * clusters, width)
    moving = jnp.transpose(velocities, (1, 0, 2)).reshape(3 * clusters, width)
    home = home_array(places, charges, atom_types, type_radius, jnp.transpose(tiles), tile_live)
    steady = home[3 * clusters : 5 * clusters]
    groups = lax.axis_size("gz")
    capacity = max(2, 2 * clusters // groups)
    slot_count = groups * capacity
    target_ids = destinations[:, 0]
    onehot = (target_ids[:, None] == jnp.arange(groups, dtype=jnp.int32)[None, :]).astype(jnp.int32)
    rank_before = jnp.cumsum(onehot, axis=0) - onehot
    position = jnp.sum(rank_before * onehot, axis=1) + target_ids * capacity
    select = (position[None, :] == jnp.arange(slot_count, dtype=jnp.int32)[:, None]).astype(jnp.float32)

    def migrated(channels):
        count = channels.shape[0] // clusters
        channels = channels.reshape(count, clusters, width)
        slots = jnp.einsum("sc,fca->fsa", select, channels, precision=lax.Precision.HIGHEST)
        slots = jnp.transpose(slots.reshape(count, groups, capacity, width), (1, 0, 2, 3))
        received = lax.all_to_all(slots, "gz", split_axis=0, concat_axis=0, tiled=True)
        return jnp.transpose(received, (1, 0, 2, 3)).reshape(count, slot_count, width)

    fixed = imported(home)
    pairs = planned(mine, clusters, tile_count, fixed[:4])
    current = fixed
    for step_index in range(STEPS):
        if step_index:
            current = imported(places)
            sent = migrated(jnp.concatenate([places, moving, steady], axis=0))
        forces = returned(tile_forces(pairs, tile_count, clusters, current, fixed))
        if not step_index:
            moving = moving + time_step * forces
            places = places + time_step * moving
    pushed = migrated(forces)
    moved = sent[3:6] + time_step * pushed
    placed = sent[0:3] + time_step * moved
    arrived = jnp.concatenate([placed, moved, sent[6:]], axis=0)
    return (jnp.transpose(forces.reshape(3, clusters, width), (1, 0, 2)), jnp.transpose(arrived, (1, 0, 2)))


def solution(mesh):
    whole = ("gz", "gy", "gx")
    placed = (
        P(whole, None, None),
        P(whole, None, None),
        P(whole, None),
        P(whole, None),
        P(),
        P(whole, None),
        P(whole),
        P(whole, None),
    )
    return jax.shard_map(
        local,
        mesh=mesh,
        in_specs=placed,
        out_specs=(P(whole, None, None), P(whole, None, None)),
        check_vma=False,
    )
```
